512 devices in a mesh: seq: 32 (over x, y, core), heads: 4 (over z_lo), dp: 4 (over z_hi).
Axes of the slice: x: 4, y: 4, z: 16 (z_hi: 4, z_lo: 4; z = z_hi * 4 + z_lo), core: 2. Of those that a mesh axis runs over, the one named last changes fastest.
Arguments:
- activations: bfloat16 [16384, 8192], P(('dp', 'seq'), 'heads'), parts along dimension 0, may hold values from -6 to 6
- conv_taps: bfloat16 [4, 8192], P(None, 'heads'), may hold values from -3 to 3
- gate_in: bfloat16 [8192, 1024], P('heads', 'seq'), may hold values from -0.0625 to 0.0625
- gate_out: bfloat16 [1024, 8], replicated, may hold values from -0.59765625 to 0.59765625
- queries: bfloat16 [16384, 8192], P(('dp', 'seq'), 'heads'), parts along dimension 0, may hold values from -1000 to 1000, as said below
- key_vectors: bfloat16 [16384, 1024], P(('dp', 'seq'), 'heads'), parts along dimension 0, may hold values from -4 to 4, as said below
- value_vectors: bfloat16 [16384, 1024], P(('dp', 'seq'), 'heads'), parts along dimension 0, may hold values from -6 to 6
- segment_ids: int32 [16384], P('dp'), parts along dimension 0, may hold values from 0 to 3, never falling along the last dimension, each value on 1 to 2048 neighbouring positions
Outputs:
- attended: bfloat16 [16384, 8192], P(('dp', 'seq'), 'heads'), parts along dimension 0
- key_mass: bfloat16 [8, 16384], P('heads', ('dp', 'seq')), parts along dimension 1
The draws below stay inside these ranges and needn't reach their ends.
There are 4 independent parts, one for each index of `dp`. The reference program is written for one: setup_inputs(seed, part) draws one part's arguments, and reference() takes and returns one part's arrays. A program takes and returns all parts, laid end to end along the dimension named above; an argument that names none is the same for every part. Nothing has to cross between parts.
Inputs may be any that keep to these rules, and one draw needn't show every extreme that they name: `queries`: finite. `key_vectors`: finite.
All inputs are finite; a program needn't handle non-finite values.
Results may differ from the reference program's by a relative error of at most 0.0056.
Values may be sent and summed in bfloat16 or wider, within the bound.
A program may use at most 64 MiB of HBM per device.

```python
import math
import jax
import jax.numpy as jnp
import numpy as np
from jax import lax

MODEL_WIDTH = 8192
QUERY_HEADS = 64
KV_HEADS = 8
HEAD_DIM = 128
GATE_HIDDEN = 1024
CONV_TAPS = 4
SEQ_LEN = 4096


def joint_draw(key):
    base_keys = jnp.clip(jax.random.normal(jax.random.fold_in(key, 21), (SEQ_LEN, KV_HEADS, HEAD_DIM), jnp.float32), -4.0, 4.0)
    base_queries = 1.5 * jnp.clip(jax.random.normal(jax.random.fold_in(key, 22), (SEQ_LEN, QUERY_HEADS, HEAD_DIM), jnp.float32), -4.0, 4.0)
    return (base_queries.reshape(SEQ_LEN, QUERY_HEADS * HEAD_DIM), base_keys.reshape(SEQ_LEN, KV_HEADS * HEAD_DIM))


def draw_queries(key, part):
    return joint_draw(key)[0].astype(jnp.bfloat16)


def draw_key_vectors(key, part):
    return joint_draw(key)[1].astype(jnp.bfloat16)


def block_scale(key, dims, pieces, least, high):
    factor_of = 1.0
    for axis_at, blocks in pieces:
        heights = jax.random.uniform(jax.random.fold_in(jax.random.fold_in(key, 6), axis_at), (blocks,), jnp.float32, least / len(pieces), high / len(pieces))
        factor_of = factor_of * jnp.repeat(jnp.exp(heights), dims[axis_at] // blocks).reshape((-1,) + (1,) * (len(dims) - 1 - axis_at))
    return factor_of


def split_up(amount, total, limit, skew):
    loads = [(1 << 20) // math.isqrt(grade ** skew) + 1 for grade in range(2, amount + 1)]
    rest, given = total - limit - (amount - 1), [1] * (amount - 1)
    while rest > 0:
        candidates = [i for i in range(amount - 1) if given[i] < limit]
        pool, left = sum([loads[i] for i in candidates]), rest
        for i in candidates:
            more = min(limit - given[i], max(1, left * loads[i] // pool), rest)
            given[i] = given[i] + more
            rest = rest - more
    return np.array([limit] + given)


def uneven(key, number_of, total, reach, lean):
    if number_of == 2:
        one = jax.random.randint(key, (), max(1, total - reach), min(reach, total - 1) + 1)
        return jnp.stack([one, total - one])
    sizes = jnp.asarray(split_up(number_of, total, reach, lean), jnp.int32)
    couples = (number_of - 1) // 2
    giver, sink = sizes[1:1 + 2 * couples:2], sizes[2:2 + 2 * couples:2]
    margin = jnp.minimum(giver - 1, reach - sink)
    moved = jax.random.randint(jax.random.fold_in(key, 1), (couples,), 0, 1 << 20) % (margin + 1)
    sizes = sizes.at[1:1 + 2 * couples:2].set(giver - moved).at[2:2 + 2 * couples:2].set(sink + moved)
    return sizes[jax.random.permutation(jax.random.fold_in(key, 2), number_of)]


def scatter_about(key, shape, scale, limit, shards=(), kind=jnp.bfloat16):
    result = scale * jax.random.normal(key, shape, jnp.float32)
    if shards:
        result = result * block_scale(key, shape, shards, -0.22, 0.18)
    return jnp.clip(result, -limit, limit).astype(kind)


def setup_inputs(seed: int = 0, part: int = 0) -> dict:
    seeds = jax.random.split(jax.random.key(seed), 9)
    part_splits = jax.random.split(jax.random.fold_in(seeds[8], part), 9)
    return {
        "activations": scatter_about(part_splits[0], (SEQ_LEN, MODEL_WIDTH), 1.0, 6.0, ((0, 32), (1, 4))),
        "conv_taps": scatter_about(seeds[1], (CONV_TAPS, MODEL_WIDTH), 0.5, 3.0, ((1, 4),)),
        "gate_in": scatter_about(seeds[2], (MODEL_WIDTH, GATE_HIDDEN), MODEL_WIDTH ** -0.5, 0.0625, ((0, 4), (1, 32))),
        "gate_out": scatter_about(seeds[3], (GATE_HIDDEN, KV_HEADS), 0.1, 0.59765625),
        "queries": draw_queries(jax.random.fold_in(jax.random.fold_in(seeds[8], part), 71), part),
        "key_vectors": draw_key_vectors(jax.random.fold_in(jax.random.fold_in(seeds[8], part), 71), part),
        "value_vectors": scatter_about(part_splits[6], (SEQ_LEN, KV_HEADS * HEAD_DIM), 1.0, 6.0, ((0, 32), (1, 4))),
        "segment_ids": jnp.searchsorted(jnp.cumsum(uneven(part_splits[7], 4, SEQ_LEN, SEQ_LEN // 2, 2)), jnp.arange(SEQ_LEN), side="right").astype(jnp.int32),
    }


def causal_mix(activations, conv_taps):
    length = activations.shape[0]
    tap_count = conv_taps.shape[0]
    widened = jnp.concatenate([jnp.zeros((tap_count - 1, activations.shape[1]), jnp.float32), activations.astype(jnp.float32)], 0)
    summed = jnp.zeros((length, activations.shape[1]), jnp.float32)
    for shift_back in range(tap_count):
        start_row = tap_count - 1 - shift_back
        summed = summed + conv_taps[shift_back].astype(jnp.float32) * widened[start_row:start_row + length]
    return summed.astype(jnp.bfloat16)

def reference(activations, conv_taps, gate_in, gate_out, queries, key_vectors, value_vectors, segment_ids):
    mixed_rows = causal_mix(activations, conv_taps)
    hidden = jax.nn.silu(jnp.dot(mixed_rows, gate_in, preferred_element_type=jnp.float32)).astype(jnp.bfloat16)
    logits = jnp.dot(hidden, gate_out, preferred_element_type=jnp.float32)
    retention = jax.nn.log_sigmoid(logits).astype(jnp.bfloat16)
    length = activations.shape[0]
    group_size = QUERY_HEADS // KV_HEADS
    score_scale = 1.0 / math.sqrt(HEAD_DIM)
    positions = jnp.arange(length, dtype=jnp.int32)
    visible = (positions[None, :] <= positions[:, None]) & (segment_ids[None, :] == segment_ids[:, None])

    def one_head(head_number):
        kv_index = head_number // group_size
        query_rows = lax.dynamic_slice_in_dim(queries, head_number * HEAD_DIM, HEAD_DIM, 1)
        key_rows = lax.dynamic_slice_in_dim(key_vectors, kv_index * HEAD_DIM, HEAD_DIM, 1)
        value_rows = lax.dynamic_slice_in_dim(value_vectors, kv_index * HEAD_DIM, HEAD_DIM, 1)
        bias_col = lax.dynamic_slice_in_dim(retention, kv_index, 1, 1)[:, 0].astype(jnp.float32)
        scores = jnp.dot(query_rows, key_rows.T, preferred_element_type=jnp.float32) * score_scale + bias_col[None, :]
        masked = jnp.where(visible, scores, -1e+30)
        row_peak = lax.optimization_barrier(jnp.max(masked, axis=1, keepdims=True))
        weights = jnp.where(visible, jnp.exp(masked - row_peak), 0.0)
        weights = weights / lax.optimization_barrier(jnp.sum(weights, axis=1, keepdims=True))
        head_out = jnp.dot(weights.astype(jnp.bfloat16), value_rows, preferred_element_type=jnp.float32).astype(jnp.bfloat16)
        return (head_out, lax.optimization_barrier(jnp.sum(weights, axis=0)))
    head_outs, column_mass = lax.map(one_head, jnp.arange(QUERY_HEADS, dtype=jnp.int32))
    attended = jnp.transpose(head_outs, (1, 0, 2)).reshape(length, QUERY_HEADS * HEAD_DIM)
    key_mass = (lax.optimization_barrier(jnp.sum(column_mass.reshape(KV_HEADS, group_size, length), axis=1)) / group_size).astype(jnp.bfloat16)
    return (attended, key_mass)
```

```python
import math

import jax
import jax.numpy as jnp
from jax import lax
from jax.experimental import pallas as pl
from jax.experimental.pallas import tpu as pltpu
from jax.sharding import PartitionSpec as P

MESH = pl.DeviceIdType.MESH
HEAD_DIM = 128
NEG = -1e30
SIDE = 4
CHIPS = SIDE * SIDE
WINDOW = 8
NT = (((1,), (1,)), ((), ()))

GATHER = 20
SEM_SWAP = 4 * GATHER
SEM_HALO = SEM_SWAP + 4
SEM_Z = SEM_HALO + 2
SEM_LOGIT = SEM_Z + 12
SEM_RET = SEM_LOGIT + 8
SEM_MASS = SEM_RET + 16
SEM_OUT = SEM_MASS + 18
SEMS = SEM_OUT + 1


def kernel(
    act_ref, taps_ref, wt_ref, gout_ref, q_ref, k_ref, v_ref, seg_ref,
    att_ref, mass_ref,
    rows_buf, mixed, wg, part, zrecv, lrecv, rown, rall, kvg, qbuf, obuf, orecv, sbuf, rel,
    colacc, colout, krecv, send_sem, recv_sem, local_sem,
):
    seq = lax.axis_index("seq")
    h = lax.axis_index("heads")
    c = lax.rem(seq, 2)
    ch = seq // 2
    x = ch // SIDE
    y = lax.rem(ch, SIDE)
    other = 1 - c
    shard_rows = act_ref.shape[0]
    half_q = q_ref.shape[1] // 2

    def at_chip(chip, core):
        return {"seq": lax.rem(chip, CHIPS) * 2 + core}

    def at_xy(xx, yy):
        return {"seq": (lax.rem(xx, SIDE) * SIDE + lax.rem(yy, SIDE)) * 2 + c}

    partner = {"seq": ch * 2 + other}

    barrier = pltpu.get_barrier_semaphore()

    def greet(i, carry):
        pl.semaphore_signal(
            barrier, inc=1, device_id={"seq": lax.rem(seq + i, 2 * CHIPS)}, device_id_type=MESH
        )
        return carry

    lax.fori_loop(1, 2 * CHIPS, greet, 0)
    for j in range(1, 4):
        for core in range(2):
            pl.semaphore_signal(
                barrier, inc=1, device_id={"seq": ch * 2 + core, "heads": lax.rem(h + j, 4)},
                device_id_type=MESH,
            )
    pl.semaphore_wait(barrier, 2 * CHIPS - 1 + 6)

    pending = []

    def send(src, dst, sem, device, rsem=None):
        copy = pltpu.make_async_remote_copy(
            src_ref=src, dst_ref=dst, send_sem=send_sem.at[sem],
            recv_sem=recv_sem.at[sem if rsem is None else rsem],
            device_id=device, device_id_type=MESH,
        )
        copy.start()
        pending.append(copy)

    def recv(slot, sem):
        pltpu.make_async_remote_copy(
            src_ref=slot, dst_ref=slot, send_sem=send_sem.at[sem], recv_sem=recv_sem.at[sem],
            device_id=partner, device_id_type=MESH,
        ).wait_recv()

    def axis_one(t, step):
        return at_xy(x + step, y) if t == 0 else at_xy(x, y + step)

    def axis_two(t, step):
        return at_xy(x, y + step) if t == 0 else at_xy(x + step, y)

    def place(t, i):
        own = x if t == 0 else y
        return lax.rem(own + (0, 3, 1, 2)[i], SIDE)

    def wslot(t, d, i, ab=None):
        p = place(t, i)
        return wg.at[:, d, t, p] if ab is None else wg.at[ab, d, t, p]

    def kvslot(t, d, i, ab=None):
        p = place(t, i)
        return kvg.at[t, d, p] if ab is None else kvg.at[t, d, p, ab]

    def second_sends(slot, base, t, i, src=None):
        source = slot(t, 0, i) if src is None else src
        sem = base + t * GATHER + 4 + 4 * i
        send(source, slot(t, 3, i), sem, axis_two(t, 1))
        send(source, slot(t, 1, i), sem + 1, axis_two(t, 3))

    def gather_start(slot, base, source):
        for t in range(2):
            sem = base + t * GATHER
            send(source(t), slot(t, 0, 0), sem, axis_one(t, 1))
            send(source(t), slot(t, 0, 0), sem + 1, axis_one(t, 3))
        for t in range(2):
            second_sends(slot, base, t, 0, source(t))

    def gather_first(slot, base):
        for t in range(2):
            sem = base + t * GATHER
            recv(slot(t, 0, 1), sem)
            send(slot(t, 0, 1, 0), slot(t, 0, 1, 0), sem + 2, axis_one(t, 1))
            recv(slot(t, 0, 2), sem + 1)
            send(slot(t, 0, 2, 1), slot(t, 0, 2, 1), sem + 3, axis_one(t, 3))
        for i in (1, 2):
            for t in range(2):
                second_sends(slot, base, t, i)
        for t in range(2):
            sem = base + t * GATHER
            recv(slot(t, 0, 3, 0), sem + 2)
            recv(slot(t, 0, 3, 1), sem + 3)
            second_sends(slot, base, t, 3)

    def gather_second(slot, base):
        for i in range(4):
            for t in range(2):
                sem = base + t * GATHER + 4 + 4 * i
                recv(slot(t, 3, i), sem)
                send(slot(t, 3, i, 0), slot(t, 2, i, 0), sem + 2, axis_two(t, 1))
                recv(slot(t, 1, i), sem + 1)
                send(slot(t, 1, i, 1), slot(t, 2, i, 1), sem + 3, axis_two(t, 3))

    def gather_last(slot, base):
        for i in range(4):
            for t in range(2):
                sem = base + t * GATHER + 4 + 4 * i
                recv(slot(t, 2, i, 0), sem + 2)
                recv(slot(t, 2, i, 1), sem + 3)

    W_BASE, KV_BASE = 0, 2 * GATHER
    gather_start(wslot, W_BASE, lambda t: wt_ref.at[t])

    own_rows = pl.ds(pl.multiple_of(c * shard_rows, 128), shard_rows)
    own_rows_in = pl.ds(pl.multiple_of(c * shard_rows + 16, 16), shard_rows)
    send(act_ref, rows_buf.at[own_rows_in], SEM_SWAP, partner)

    @pl.when(c == 1)
    def _():
        for core in range(2):
            pltpu.make_async_remote_copy(
                src_ref=act_ref.at[shard_rows - 16 : shard_rows], dst_ref=rows_buf.at[0:16],
                send_sem=send_sem.at[SEM_HALO + core], recv_sem=recv_sem.at[SEM_HALO],
                device_id=at_chip(ch + 1, core), device_id_type=MESH,
            ).start()

    def columns(which, width):
        return pl.ds(pl.multiple_of(which * width, width), width)

    send(k_ref.at[:, columns(other, 128)], kvg.at[0, 0, x, c], SEM_SWAP + 2, partner)
    send(v_ref.at[:, columns(other, 128)], kvg.at[1, 0, y, c], SEM_SWAP + 3, partner)
    send(q_ref.at[:, columns(other, half_q)], qbuf.at[own_rows], SEM_SWAP + 1, partner)
    local = [
        pltpu.make_async_copy(act_ref, rows_buf.at[own_rows_in], local_sem.at[0]),
        pltpu.make_async_copy(wt_ref.at[0], wslot(0, 0, 0), local_sem.at[1]),
        pltpu.make_async_copy(wt_ref.at[1], wslot(1, 0, 0), local_sem.at[2]),
        pltpu.make_async_copy(k_ref.at[:, columns(c, 128)], kvg.at[0, 0, x, c], local_sem.at[3]),
        pltpu.make_async_copy(v_ref.at[:, columns(c, 128)], kvg.at[1, 0, y, c], local_sem.at[4]),
        pltpu.make_async_copy(q_ref.at[:, columns(c, half_q)], qbuf.at[own_rows], local_sem.at[5]),
    ]
    for copy in local:
        copy.start()

    gather_first(wslot, W_BASE)

    recv(rows_buf.at[0:16], SEM_HALO)
    recv(rows_buf.at[pl.ds(pl.multiple_of(other * shard_rows + 16, 16), shard_rows)], SEM_SWAP)
    for copy in local:
        copy.wait()

    @pl.when(ch == 0)
    def _():
        rows_buf[0:16, :] = jnp.zeros((16, rows_buf.shape[1]), jnp.bfloat16)

    width = 512
    tap_count = taps_ref.shape[0]

    def mix(step, carry):
        r0 = pl.multiple_of((step // 4) * 64, 64)
        cols = pl.ds(pl.multiple_of(lax.rem(step, 4) * width, width), width)
        block = rows_buf[pl.ds(r0, 80), cols].astype(jnp.float32)
        total = jnp.zeros((64, width), jnp.float32)
        for tap in range(tap_count):
            moved = block if tap == 0 else pltpu.roll(block, tap, axis=0)
            total = total + taps_ref[tap : tap + 1, cols].astype(jnp.float32) * moved[16:80]
        mixed[pl.ds(r0, 64), cols] = total.astype(jnp.bfloat16)
        return carry

    lax.fori_loop(0, (2 * shard_rows // 64) * (mixed.shape[1] // width), mix, 0)

    def gate_group(d):
        depth = mixed.shape[1] // 2
        total = None
        for ab in range(2):
            term = lax.dot_general(
                mixed[:, ab * depth : (ab + 1) * depth],
                wg[ab, d].reshape(128, depth), NT, preferred_element_type=jnp.float32,
            )
            total = term if total is None else total + term
        part[d] = total
        for j in range(1, 4):
            peer = lax.rem(h + j, 4)
            send(
                part.at[d, pl.ds(pl.multiple_of(peer * 64, 64), 64)], zrecv.at[d, j - 1],
                SEM_Z + 3 * d + j - 1, {"heads": peer},
            )

    gate_group(0)
    gather_second(wslot, W_BASE)

    recv(kvg.at[0, 0, x, other], SEM_SWAP + 2)
    recv(kvg.at[1, 0, y, other], SEM_SWAP + 3)
    gather_start(kvslot, KV_BASE, lambda t: kvslot(t, 0, 0))

    gate_group(3)
    gate_group(1)
    gather_last(wslot, W_BASE)
    gate_group(2)

    gather_first(kvslot, KV_BASE)

    logits = jnp.zeros((8, 64), jnp.float32)
    for d in (0, 3, 1, 2):
        for j in range(3):
            recv(zrecv.at[d, j], SEM_Z + 3 * d + j)
        pre = part[d, pl.ds(pl.multiple_of(h * 64, 64), 64), :]
        pre = pre + zrecv[d, 0] + zrecv[d, 1] + zrecv[d, 2]
        hidden = (pre / (1.0 + jnp.exp(-pre))).astype(jnp.bfloat16)
        gout = gout_ref[c, 0, lax.rem(y + d, SIDE)] + gout_ref[c, 1, lax.rem(x + d, SIDE)]
        logits = logits + lax.dot_general(gout, hidden, NT, preferred_element_type=jnp.float32)
    mine = 2 * h + c
    lrecv[mine] = jnp.concatenate([logits, jnp.zeros((8, 64), jnp.float32)], 1)
    for j in range(4):
        for flip in range(2):
            if j or flip:
                peer, core = lax.rem(h + j, 4), lax.rem(c + flip, 2)
                send(
                    lrecv.at[mine], lrecv.at[mine], SEM_LOGIT + 2 * j + flip,
                    {"seq": ch * 2 + core, "heads": peer},
                )

    gather_second(kvslot, KV_BASE)

    for j in range(4):
        for flip in range(2):
            if j or flip:
                peer, core = lax.rem(h + 4 - j, 4), lax.rem(c + flip, 2)
                recv(lrecv.at[2 * peer + core], SEM_LOGIT + 2 * j + flip)
    lane = lax.broadcasted_iota(jnp.int32, (8, 128), 1)
    for block in range(2):
        low = lrecv[4 * block] + lrecv[4 * block + 1]
        high = pltpu.roll(lrecv[4 * block + 2] + lrecv[4 * block + 3], 64, axis=1)
        value = jnp.where(lane < 64, low, high)
        sig = jnp.minimum(value, 0.0) - jnp.log1p(jnp.exp(-jnp.abs(value)))
        rown[block] = sig.astype(jnp.bfloat16).astype(jnp.float32)
    for block in range(2):
        rall[ch, block : block + 1, :] = rown[block, pl.ds(mine, 1), :]
    for i in range(1, CHIPS):
        send(rall.at[ch], rall.at[ch], SEM_RET + i, at_chip(ch + i, c))

    gather_last(kvslot, KV_BASE)
    recv(qbuf.at[pl.ds(pl.multiple_of(other * shard_rows, 128), shard_rows)], SEM_SWAP + 1)

    rows = 2 * shard_rows
    pos = (ch * rows + lax.broadcasted_iota(jnp.int32, (rows, rows), 0)).astype(jnp.float32)
    first = jnp.zeros((rows, rows), jnp.float32)
    seg = seg_ref[...]
    for number in range(1, 4):
        count = jnp.sum((seg < number).astype(jnp.float32), axis=1, keepdims=True)
        count = jnp.sum(count, axis=0, keepdims=True)
        first = jnp.where(pos >= count, jnp.maximum(first, count), first)
    rel[...] = first - lax.broadcasted_iota(jnp.int32, (rows, rows), 1).astype(jnp.float32)
    colacc[...] = jnp.zeros_like(colacc)

    for i in range(1, CHIPS):
        recv(rall.at[lax.rem(ch + CHIPS - i, CHIPS)], SEM_RET + i)

    scale = 1.0 / math.sqrt(HEAD_DIM)
    blocks = range(WINDOW + 1)

    def chip_of(b):
        return lax.rem(ch + CHIPS - WINDOW + b, CHIPS)

    def head(e, carry):
        cols = pl.ds(pl.multiple_of(e * HEAD_DIM, HEAD_DIM), HEAD_DIM)
        query = qbuf[:, cols]
        peak = jnp.full((rows, 128), NEG, jnp.float32)
        for b in blocks:
            chip = chip_of(b)
            kx, ky = chip // SIDE, lax.rem(chip, SIDE)
            keys = kvg[0, lax.rem(ky + SIDE - y, SIDE), kx].reshape(rows, HEAD_DIM)
            bias = rall[chip]
            scores = lax.dot_general(query, keys, NT, preferred_element_type=jnp.float32) * scale
            start = ((ch - WINDOW + b) * rows).astype(jnp.float32)
            for half in range(2):
                lanes = slice(128 * half, 128 * half + 128)
                piece = scores[:, lanes] + bias[half : half + 1]
                seen = rel[:, lanes] <= start
                if b == WINDOW:
                    seen = seen & (
                        lax.broadcasted_iota(jnp.int32, (rows, 128), 1) + 128 * half
                        <= lax.broadcasted_iota(jnp.int32, (rows, 128), 0)
                    )
                piece = jnp.where(seen, piece, NEG)
                sbuf[b, :, lanes] = piece
                peak = jnp.maximum(peak, piece)
        top = jnp.max(peak, axis=1, keepdims=True)
        mass = jnp.zeros((rows, 128), jnp.float32)
        for b in blocks:
            for half in range(2):
                lanes = slice(128 * half, 128 * half + 128)
                piece = jnp.exp(sbuf[b, :, lanes] - top)
                sbuf[b, :, lanes] = piece
                mass = mass + piece
        inverse = 1.0 / jnp.sum(mass, axis=1, keepdims=True)
        out = jnp.zeros((rows, HEAD_DIM), jnp.float32)
        for b in blocks:
            chip = chip_of(b)
            kx, ky = chip // SIDE, lax.rem(chip, SIDE)
            values = kvg[1, lax.rem(kx + SIDE - x, SIDE), ky].reshape(rows, HEAD_DIM)
            weights = sbuf[b] * inverse
            colacc[b] += jnp.sum(weights.reshape(rows // 8, 8, rows), axis=0)
            out = out + jnp.dot(
                weights.astype(jnp.bfloat16), values, preferred_element_type=jnp.float32
            )
        obuf[:, cols] = out.astype(jnp.bfloat16)
        return carry

    lax.fori_loop(0, half_q // HEAD_DIM, head, 0)

    their_rows = pl.ds(pl.multiple_of(other * shard_rows, 128), shard_rows)
    for b in blocks:
        total = jnp.sum(colacc[b], axis=0, keepdims=True)
        for half in range(2):
            colout[b, half] = total[:, 128 * half : 128 * half + 128]
    for b in range(WINDOW):
        for half in range(2):
            send(
                colout.at[b, half], krecv.at[b, c], SEM_MASS + 2 * b + half,
                at_chip(ch + CHIPS - WINDOW + b, half), SEM_MASS + 2 * b + c,
            )
    send(
        colout.at[WINDOW, other], krecv.at[WINDOW, c], SEM_MASS + 2 * WINDOW + other, partner,
        SEM_MASS + 2 * WINDOW + c,
    )
    krecv[WINDOW, c] = colout[WINDOW, c]
    send(obuf.at[their_rows], orecv, SEM_OUT, partner)
    keep = pltpu.make_async_copy(
        obuf.at[own_rows], att_ref.at[:, columns(c, half_q)], local_sem.at[0]
    )
    keep.start()
    recv(orecv, SEM_OUT)
    put = pltpu.make_async_copy(orecv, att_ref.at[:, columns(other, half_q)], local_sem.at[1])
    put.start()

    for b in range(WINDOW):
        for core in range(2):
            recv(krecv.at[b, core], SEM_MASS + 2 * b + core)
    recv(krecv.at[WINDOW, other], SEM_MASS + 2 * WINDOW + other)
    for core in range(2):
        total = krecv[0, core]
        for b in range(1, WINDOW + 1):
            total = total + krecv[b, core]
        mass_ref[core : core + 1, :] = (total / 8.0).astype(jnp.bfloat16)

    keep.wait()
    put.wait()
    for copy in pending:
        copy.wait_send()

    @pl.when(c == 1)
    def _():
        for core in range(2):
            pltpu.make_async_remote_copy(
                src_ref=act_ref.at[shard_rows - 16 : shard_rows], dst_ref=rows_buf.at[0:16],
                send_sem=send_sem.at[SEM_HALO + core], recv_sem=recv_sem.at[SEM_HALO],
                device_id=at_chip(ch + 1, core), device_id_type=MESH,
            ).wait_send()


def per_device(
    activations, conv_taps, gate_in, gate_out, queries, key_vectors, value_vectors, segment_ids
):
    rows, features = activations.shape
    depth = features // 2
    wt = gate_in.T.reshape(2, 16, 2, depth).transpose(0, 2, 1, 3)
    units = gate_out.reshape(SIDE, SIDE, 2, 2, 16, 8)
    by_y = units[:, :, :, 0].transpose(2, 1, 4, 0, 3).reshape(2, SIDE, 8, 64)
    by_x = units[:, :, :, 1].transpose(2, 0, 4, 1, 3).reshape(2, SIDE, 8, 64)
    none = jnp.zeros_like(by_y)
    gout = jnp.stack(
        [jnp.concatenate([by_y, none], 3), jnp.concatenate([none, by_x], 3)], axis=1
    )
    seg = segment_ids.reshape(-1, 128)
    width = queries.shape[1] // 2
    vmem = pl.BlockSpec(memory_space=pltpu.VMEM)
    anywhere = pl.BlockSpec(memory_space=pl.ANY)
    both = 2 * rows
    bf16, f32 = jnp.bfloat16, jnp.float32
    return pl.pallas_call(
        kernel,
        name="retention_step",
        out_shape=(
            jax.ShapeDtypeStruct((rows, 2 * width), bf16),
            jax.ShapeDtypeStruct((2, rows), bf16),
        ),
        in_specs=[anywhere, vmem, anywhere, vmem, anywhere, anywhere, anywhere, vmem],
        out_specs=(anywhere, vmem),
        scratch_shapes=[
            pltpu.VMEM((both + 16, features), bf16),
            pltpu.VMEM((both, features), bf16),
            pltpu.VMEM((2, SIDE, 2, SIDE, 16, depth), bf16),
            pltpu.VMEM((SIDE, both, 128), f32),
            pltpu.VMEM((SIDE, 3, 64, 128), f32),
            pltpu.VMEM((8, 8, 128), f32),
            pltpu.VMEM((2, 8, 128), f32),
            pltpu.VMEM((CHIPS, 2, 128), f32),
            pltpu.VMEM((2, SIDE, SIDE, 2, rows, HEAD_DIM), bf16),
            pltpu.VMEM((both, width), bf16),
            pltpu.VMEM((both, width), bf16),
            pltpu.VMEM((rows, width), bf16),
            pltpu.VMEM((WINDOW + 1, both, both), f32),
            pltpu.VMEM((both, both), f32),
            pltpu.VMEM((WINDOW + 1, 8, both), f32),
            pltpu.VMEM((WINDOW + 1, 2, 1, 128), f32),
            pltpu.VMEM((WINDOW + 1, 2, 1, 128), f32),
            pltpu.SemaphoreType.DMA((SEMS,)),
            pltpu.SemaphoreType.DMA((SEMS,)),
            pltpu.SemaphoreType.DMA((6,)),
        ],
        compiler_params=pltpu.CompilerParams(collective_id=0, has_side_effects=True),
    )(activations, conv_taps, wt, gout, queries, key_vectors, value_vectors, seg)


def solution(mesh):
    return jax.shard_map(
        per_device,
        mesh=mesh,
        in_specs=(
            P(("dp", "seq"), "heads"),
            P(None, "heads"),
            P("heads", "seq"),
            P(),
            P(("dp", "seq"), "heads"),
            P(("dp", "seq"), "heads"),
            P(("dp", "seq"), "heads"),
            P("dp"),
        ),
        out_specs=(P(("dp", "seq"), "heads"), P("heads", ("dp", "seq"))),
        check_vma=False,
    )
```

```python
import math

import jax
import jax.numpy as jnp
from jax import lax
from jax.experimental import pallas as pl
from jax.experimental.pallas import tpu as pltpu
from jax.sharding import PartitionSpec as P

MESH = pl.DeviceIdType.MESH
HEAD_DIM = 128
NEG = -1e30
LOG2E = math.log2(math.e)
SIDE = 4
CHIPS = SIDE * SIDE
WINDOW = 8
NT = (((1,), (1,)), ((), ()))

GATHER = 20
SEM_SWAP = 4 * GATHER
SEM_HALO = SEM_SWAP + 4
SEM_Z = SEM_HALO + 2
SEM_LOGIT = SEM_Z + 12
SEM_RET = SEM_LOGIT + 8
SEM_MASS = SEM_RET + 16
SEM_OUT = SEM_MASS + 18
SEMS = SEM_OUT + 8


def kernel(
    act_ref, taps_ref, wt_ref, gout_ref, q_ref, k_ref, v_ref, seg_ref,
    att_ref, mass_ref,
    rows_buf, mixed, wg, part, gsel, zrecv, lrecv, rown, rall, kvg, qbuf, obuf, orecv, sbuf, tbuf, tops, rel,
    colacc, colout, krecv, added, send_sem, recv_sem, local_sem,
):
    seq = lax.axis_index("seq")
    h = lax.axis_index("heads")
    c = lax.rem(seq, 2)
    ch = seq // 2
    x = ch // SIDE
    y = lax.rem(ch, SIDE)
    other = 1 - c
    shard_rows = act_ref.shape[0]
    half_q = q_ref.shape[1] // 2
    depth = act_ref.shape[1] // 2

    def at_chip(chip, core):
        return {"seq": lax.rem(chip, CHIPS) * 2 + core}

    def at_xy(xx, yy):
        return {"seq": (lax.rem(xx, SIDE) * SIDE + lax.rem(yy, SIDE)) * 2 + c}

    partner = {"seq": ch * 2 + other}

    barrier = pltpu.get_barrier_semaphore()

    def greet(i, carry):
        pl.semaphore_signal(
            barrier, inc=1, device_id={"seq": lax.rem(seq + i, 2 * CHIPS)}, device_id_type=MESH
        )
        return carry

    lax.fori_loop(1, 2 * CHIPS, greet, 0)
    for j in range(1, 4):
        for core in range(2):
            pl.semaphore_signal(
                barrier, inc=1, device_id={"seq": ch * 2 + core, "heads": lax.rem(h + j, 4)},
                device_id_type=MESH,
            )
    def columns(which, width):
        return pl.ds(pl.multiple_of(which * width, width), width)

    own_rows = pl.ds(pl.multiple_of(c * shard_rows, 128), shard_rows)
    own_rows_in = pl.ds(pl.multiple_of(c * shard_rows + 16, 16), shard_rows)

    def place(t, i):
        own = x if t == 0 else y
        return lax.rem(own + (0, 3, 1, 2)[i], SIDE)

    def wslot(t, d, i, ab=None):
        p = place(t, i)
        if ab is None:
            return wg.at[d, t, p]
        return wg.at[d, t, p, :, ab * depth : (ab + 1) * depth]

    def kvslot(t, d, i, ab=None):
        p = place(t, i)
        return kvg.at[t, d, p] if ab is None else kvg.at[t, d, p, ab]

    local = [
        pltpu.make_async_copy(act_ref, rows_buf.at[own_rows_in], local_sem.at[0]),
        pltpu.make_async_copy(wt_ref.at[0:16], wslot(0, 0, 0), local_sem.at[1]),
        pltpu.make_async_copy(wt_ref.at[16:32], wslot(1, 0, 0), local_sem.at[2]),
        pltpu.make_async_copy(k_ref.at[:, columns(c, 128)], kvg.at[0, 0, x, c], local_sem.at[3]),
        pltpu.make_async_copy(v_ref.at[:, columns(c, 128)], kvg.at[1, 0, y, c], local_sem.at[4]),
        pltpu.make_async_copy(q_ref.at[:, columns(c, half_q)], qbuf.at[own_rows], local_sem.at[5]),
    ]
    for copy in local:
        copy.start()

    rows = 2 * shard_rows
    pos = (ch * rows + lax.broadcasted_iota(jnp.int32, (rows, rows), 0)).astype(jnp.float32)
    first = jnp.zeros((rows, rows), jnp.float32)
    seg = seg_ref[...]
    for number in range(1, 4):
        count = jnp.sum((seg < number).astype(jnp.float32), axis=1, keepdims=True)
        count = jnp.sum(count, axis=0, keepdims=True)
        first = jnp.where(pos >= count, jnp.maximum(first, count), first)
    rel[...] = first - lax.broadcasted_iota(jnp.int32, (rows, rows), 1).astype(jnp.float32)
    colacc[...] = jnp.zeros_like(colacc)

    lane = lax.broadcasted_iota(jnp.int32, (1, 128), 1)
    kind, which, unit = lane // 64, lax.rem(lane // 16, SIDE), lax.rem(lane, 16)
    for d in range(SIDE):
        place_x = jnp.where(kind == 0, which, lax.rem(x + d, SIDE))
        place_y = jnp.where(kind == 0, lax.rem(y + d, SIDE), which)
        column = ((place_x * SIDE + place_y) * 2 + c) * 32 + kind * 16 + unit
        pick = lax.broadcasted_iota(jnp.int32, (gout_ref.shape[1], 128), 0) == column
        pick = jnp.where(pick, 1.0, 0.0).astype(jnp.bfloat16)
        chosen = jnp.dot(gout_ref[...], pick, preferred_element_type=jnp.float32)
        gsel[d] = chosen.astype(jnp.bfloat16)

    pl.semaphore_wait(barrier, 2 * CHIPS - 1 + 6)

    pending = []

    def send(src, dst, sem, device, rsem=None):
        copy = pltpu.make_async_remote_copy(
            src_ref=src, dst_ref=dst, send_sem=send_sem.at[sem],
            recv_sem=recv_sem.at[sem if rsem is None else rsem],
            device_id=device, device_id_type=MESH,
        )
        copy.start()
        pending.append(copy)

    def recv(slot, sem):
        pltpu.make_async_remote_copy(
            src_ref=slot, dst_ref=slot, send_sem=send_sem.at[sem], recv_sem=recv_sem.at[sem],
            device_id=partner, device_id_type=MESH,
        ).wait_recv()

    def axis_one(t, step):
        return at_xy(x + step, y) if t == 0 else at_xy(x, y + step)

    def axis_two(t, step):
        return at_xy(x, y + step) if t == 0 else at_xy(x + step, y)

    def second_sends(slot, base, t, i, src=None):
        source = slot(t, 0, i) if src is None else src
        sem = base + t * GATHER + 4 + 4 * i
        send(source, slot(t, 3, i), sem, axis_two(t, 1))
        send(source, slot(t, 1, i), sem + 1, axis_two(t, 3))

    def gather_start(slot, base, source):
        for t in range(2):
            sem = base + t * GATHER
            send(source(t), slot(t, 0, 0), sem, axis_one(t, 1))
            send(source(t), slot(t, 0, 0), sem + 1, axis_one(t, 3))
        for t in range(2):
            second_sends(slot, base, t, 0, source(t))

    def gather_first(slot, base):
        for t in range(2):
            sem = base + t * GATHER
            recv(slot(t, 0, 1), sem)
            send(slot(t, 0, 1, 0), slot(t, 0, 1, 0), sem + 2, axis_one(t, 1))
            recv(slot(t, 0, 2), sem + 1)
            send(slot(t, 0, 2, 1), slot(t, 0, 2, 1), sem + 3, axis_one(t, 3))
        for i in (1, 2):
            for t in range(2):
                second_sends(slot, base, t, i)
        for t in range(2):
            sem = base + t * GATHER
            recv(slot(t, 0, 3, 0), sem + 2)
            recv(slot(t, 0, 3, 1), sem + 3)
            second_sends(slot, base, t, 3)

    def gather_second(slot, base):
        for i in range(4):
            for t in range(2):
                sem = base + t * GATHER + 4 + 4 * i
                recv(slot(t, 3, i), sem)
                send(slot(t, 3, i, 0), slot(t, 2, i, 0), sem + 2, axis_two(t, 1))
                recv(slot(t, 1, i), sem + 1)
                send(slot(t, 1, i, 1), slot(t, 2, i, 1), sem + 3, axis_two(t, 3))

    def gather_last(slot, base):
        for i in range(4):
            for t in range(2):
                sem = base + t * GATHER + 4 + 4 * i
                recv(slot(t, 2, i, 0), sem + 2)
                recv(slot(t, 2, i, 1), sem + 3)

    W_BASE, KV_BASE = 0, 2 * GATHER
    gather_start(wslot, W_BASE, lambda t: wt_ref.at[16 * t : 16 * t + 16])

    send(act_ref, rows_buf.at[own_rows_in], SEM_SWAP, partner)

    @pl.when((c == 1) & (ch < CHIPS - 1))
    def _():
        for core in range(2):
            pltpu.make_async_remote_copy(
                src_ref=act_ref.at[shard_rows - 16 : shard_rows], dst_ref=rows_buf.at[0:16],
                send_sem=send_sem.at[SEM_HALO + core], recv_sem=recv_sem.at[SEM_HALO],
                device_id=at_chip(ch + 1, core), device_id_type=MESH,
            ).start()

    send(k_ref.at[:, columns(other, 128)], kvg.at[0, 0, x, c], SEM_SWAP + 2, partner)
    send(v_ref.at[:, columns(other, 128)], kvg.at[1, 0, y, c], SEM_SWAP + 3, partner)
    send(q_ref.at[:, columns(other, half_q)], qbuf.at[own_rows], SEM_SWAP + 1, partner)
    gather_first(wslot, W_BASE)

    @pl.when(ch > 0)
    def _():
        recv(rows_buf.at[0:16], SEM_HALO)

    recv(rows_buf.at[pl.ds(pl.multiple_of(other * shard_rows + 16, 16), shard_rows)], SEM_SWAP)
    for copy in local:
        copy.wait()

    @pl.when(ch == 0)
    def _():
        rows_buf[0:16, :] = jnp.zeros((16, rows_buf.shape[1]), jnp.bfloat16)

    width = 512
    tap_count = taps_ref.shape[0]

    def mix(step, carry):
        r0 = pl.multiple_of((step // 4) * 64, 64)
        cols = pl.ds(pl.multiple_of(lax.rem(step, 4) * width, width), width)
        block = rows_buf[pl.ds(r0, 80), cols].astype(jnp.float32)
        total = jnp.zeros((64, width), jnp.float32)
        for tap in range(tap_count):
            moved = block if tap == 0 else pltpu.roll(block, tap, axis=0)
            total = total + taps_ref[tap : tap + 1, cols].astype(jnp.float32) * moved[16:80]
        mixed[pl.ds(r0, 64), cols] = total.astype(jnp.bfloat16)
        return carry

    lax.fori_loop(0, (2 * shard_rows // 64) * (mixed.shape[1] // width), mix, 0)

    def gate_group(d):
        total = lax.dot_general(
            mixed[...], wg[d].reshape(128, mixed.shape[1]), NT, preferred_element_type=jnp.float32
        )
        part[d] = total
        for j in range(1, 4):
            peer = lax.rem(h + j, 4)
            send(
                part.at[d, pl.ds(pl.multiple_of(peer * 64, 64), 64)], zrecv.at[d, j - 1],
                SEM_Z + 3 * d + j - 1, {"heads": peer},
            )

    gate_group(0)
    gather_second(wslot, W_BASE)

    recv(kvg.at[0, 0, x, other], SEM_SWAP + 2)
    recv(kvg.at[1, 0, y, other], SEM_SWAP + 3)
    gather_start(kvslot, KV_BASE, lambda t: kvslot(t, 0, 0))

    gate_group(3)
    gate_group(1)
    gather_last(wslot, W_BASE)
    gate_group(2)

    gather_first(kvslot, KV_BASE)

    logits = jnp.zeros((8, 64), jnp.float32)
    for d in (0, 3, 1, 2):
        for j in range(3):
            recv(zrecv.at[d, j], SEM_Z + 3 * d + j)
        pre = part[d, pl.ds(pl.multiple_of(h * 64, 64), 64), :]
        for j in range(3):
            pre = pre + zrecv[d, j]
        hidden = (pre / (1.0 + jnp.exp(-pre))).astype(jnp.bfloat16)
        logits = logits + lax.dot_general(gsel[d], hidden, NT, preferred_element_type=jnp.float32)
    mine = 2 * h + c
    lrecv[mine] = jnp.concatenate([logits, jnp.zeros((8, 64), jnp.float32)], 1)
    for j in range(4):
        for flip in range(2):
            if j or flip:
                peer, core = lax.rem(h + j, 4), lax.rem(c + flip, 2)
                send(
                    lrecv.at[mine], lrecv.at[mine], SEM_LOGIT + 2 * j + flip,
                    {"seq": ch * 2 + core, "heads": peer},
                )

    gather_second(kvslot, KV_BASE)

    for j in range(4):
        for flip in range(2):
            if j or flip:
                peer, core = lax.rem(h + 4 - j, 4), lax.rem(c + flip, 2)
                recv(lrecv.at[2 * peer + core], SEM_LOGIT + 2 * j + flip)
    lane = lax.broadcasted_iota(jnp.int32, (8, 128), 1)
    for block in range(2):
        low = lrecv[4 * block] + lrecv[4 * block + 1]
        high = pltpu.roll(lrecv[4 * block + 2] + lrecv[4 * block + 3], 64, axis=1)
        value = jnp.where(lane < 64, low, high)
        sig = jnp.minimum(value, 0.0) - jnp.log1p(jnp.exp(-jnp.abs(value)))
        rown[block] = sig.astype(jnp.bfloat16).astype(jnp.float32)
    for block in range(2):
        rall[ch, block : block + 1, :] = rown[block, pl.ds(mine, 1), :]
    for i in range(1, CHIPS):
        send(rall.at[ch], rall.at[ch], SEM_RET + i, at_chip(ch + i, c))

    gather_last(kvslot, KV_BASE)
    recv(qbuf.at[pl.ds(pl.multiple_of(other * shard_rows, 128), shard_rows)], SEM_SWAP + 1)

    for copy in pending:
        copy.wait_send()
    pending.clear()

    for i in range(1, CHIPS):
        recv(rall.at[lax.rem(ch + CHIPS - i, CHIPS)], SEM_RET + i)

    scale = LOG2E / math.sqrt(HEAD_DIM)
    blocks = range(WINDOW + 1)

    def chip_of(b):
        return lax.rem(ch + CHIPS - WINDOW + b, CHIPS)

    for b in blocks:
        bias = rall[chip_of(b)] * LOG2E
        start = ((ch - WINDOW + b) * rows).astype(jnp.float32)
        for half in range(2):
            lanes = slice(128 * half, 128 * half + 128)
            seen = rel[:, lanes] <= start
            if b == WINDOW:
                seen = seen & (
                    lax.broadcasted_iota(jnp.int32, (rows, 128), 1) + 128 * half
                    <= lax.broadcasted_iota(jnp.int32, (rows, 128), 0)
                )
            added[b, :, lanes] = jnp.where(seen, bias[half : half + 1], NEG)

    their_rows = pl.ds(pl.multiple_of(other * shard_rows, 128), shard_rows)

    def give(e):
        return pltpu.make_async_remote_copy(
            src_ref=obuf.at[e, their_rows], dst_ref=orecv.at[e],
            send_sem=send_sem.at[SEM_OUT + e], recv_sem=recv_sem.at[SEM_OUT + e],
            device_id=partner, device_id_type=MESH,
        )

    def key_block(kind, b):
        chip = chip_of(b)
        kx, ky = chip // SIDE, lax.rem(chip, SIDE)
        if kind == 0:
            block = kvg[0, lax.rem(ky + SIDE - y, SIDE), kx]
        else:
            block = kvg[1, lax.rem(kx + SIDE - x, SIDE), ky]
        return block.reshape(rows, HEAD_DIM)

    def query_of(e):
        return qbuf[:, pl.ds(pl.multiple_of(e * HEAD_DIM, HEAD_DIM), HEAD_DIM)]

    def score(query, slot, b, peak):
        scores = lax.dot_general(query, key_block(0, b), NT, preferred_element_type=jnp.float32)
        scores = scores * scale + added[b]
        slot[b] = scores
        return jnp.maximum(peak, jnp.maximum(scores[:, :128], scores[:, 128:]))

    def soften(slot, b, top, mass):
        piece = jnp.exp2(slot[b] - top)
        slot[b] = piece
        return mass + (piece[:, :128] + piece[:, 128:])

    def spread(slot, b, inverse, out):
        weights = slot[b] * inverse
        colacc[b] += jnp.sum(weights.reshape(rows // 8, 8, rows), axis=0)
        return out + jnp.dot(
            weights.astype(jnp.bfloat16), key_block(1, b), preferred_element_type=jnp.float32
        )

    low = jnp.full((rows, 128), NEG, jnp.float32)
    none = jnp.zeros((rows, 128), jnp.float32)

    def finish(e, slot, inverse):
        out = none
        for b in blocks:
            out = spread(slot, b, inverse, out)
        obuf[e] = out.astype(jnp.bfloat16)
        give(e).start()

    def widest(peak):
        tops[...] = jnp.broadcast_to(jnp.max(peak, axis=1, keepdims=True), (rows, 128))

    peak = low
    query = query_of(0)
    for b in blocks:
        peak = score(query, sbuf, b, peak)
    widest(peak)
    head_count = half_q // HEAD_DIM

    def head_pair(pair, carry):
        for i, slot, following in ((0, sbuf, tbuf), (1, tbuf, sbuf)):
            e = 2 * pair + i
            top = tops[:, :1]
            query = query_of(jnp.minimum(e + 1, head_count - 1))
            peak, mass = low, none
            for b in blocks:
                peak = score(query, following, b, peak)
                mass = soften(slot, b, top, mass)
            finish(e, slot, 1.0 / jnp.sum(mass, axis=1, keepdims=True))
            widest(peak)
        return carry

    lax.fori_loop(0, head_count // 2, head_pair, 0)

    for b in blocks:
        total = jnp.sum(colacc[b], axis=0, keepdims=True)
        for half in range(2):
            colout[b, half] = total[:, 128 * half : 128 * half + 128]
    for b in range(WINDOW):
        for half in range(2):
            send(
                colout.at[b, half], krecv.at[b, c], SEM_MASS + 2 * b + half,
                at_chip(ch + CHIPS - WINDOW + b, half), SEM_MASS + 2 * b + c,
            )
    send(
        colout.at[WINDOW, other], krecv.at[WINDOW, c], SEM_MASS + 2 * WINDOW + other, partner,
        SEM_MASS + 2 * WINDOW + c,
    )
    krecv[WINDOW, c] = colout[WINDOW, c]
    heads = range(half_q // HEAD_DIM)
    puts = []

    def put(source, e, sem):
        copy = pltpu.make_async_copy(source, att_ref.at[:, columns(e, HEAD_DIM)], local_sem.at[sem])
        copy.start()
        puts.append(copy)

    for e in heads:
        put(obuf.at[e, own_rows], 8 * c + e, e)
    for e in heads:
        give(e).wait()
        put(orecv.at[e], 8 * other + e, 8 + e)

    for b in range(WINDOW):
        for core in range(2):
            recv(krecv.at[b, core], SEM_MASS + 2 * b + core)
    recv(krecv.at[WINDOW, other], SEM_MASS + 2 * WINDOW + other)
    for core in range(2):
        total = krecv[0, core]
        for b in range(1, WINDOW + 1):
            total = total + krecv[b, core]
        mass_ref[core : core + 1, :] = (total / 8.0).astype(jnp.bfloat16)

    for copy in puts:
        copy.wait()
    for copy in pending:
        copy.wait_send()

    @pl.when((c == 1) & (ch < CHIPS - 1))
    def _():
        for core in range(2):
            pltpu.make_async_remote_copy(
                src_ref=act_ref.at[shard_rows - 16 : shard_rows], dst_ref=rows_buf.at[0:16],
                send_sem=send_sem.at[SEM_HALO + core], recv_sem=recv_sem.at[SEM_HALO],
                device_id=at_chip(ch + 1, core), device_id_type=MESH,
            ).wait_send()


def per_device(
    activations, conv_taps, gate_in, gate_out, queries, key_vectors, value_vectors, segment_ids
):
    rows, features = activations.shape
    seg = segment_ids.reshape(-1, 128)
    width = queries.shape[1] // 2
    vmem = pl.BlockSpec(memory_space=pltpu.VMEM)
    anywhere = pl.BlockSpec(memory_space=pl.ANY)
    both = 2 * rows
    bf16, f32 = jnp.bfloat16, jnp.float32
    return pl.pallas_call(
        kernel,
        name="retention_step",
        out_shape=(
            jax.ShapeDtypeStruct((rows, 2 * width), bf16),
            jax.ShapeDtypeStruct((2, rows), bf16),
        ),
        in_specs=[anywhere, vmem, anywhere, vmem, anywhere, anywhere, anywhere, vmem],
        out_specs=(anywhere, vmem),
        scratch_shapes=[
            pltpu.VMEM((both + 16, features), bf16),
            pltpu.VMEM((both, features), bf16),
            pltpu.VMEM((SIDE, 2, SIDE, 16, features), bf16),
            pltpu.VMEM((SIDE, both, 128), f32),
            pltpu.VMEM((SIDE, 8, 128), bf16),
            pltpu.VMEM((SIDE, 3, 64, 128), f32),
            pltpu.VMEM((8, 8, 128), f32),
            pltpu.VMEM((2, 8, 128), f32),
            pltpu.VMEM((CHIPS, 2, 128), f32),
            pltpu.VMEM((2, SIDE, SIDE, 2, rows, HEAD_DIM), bf16),
            pltpu.VMEM((both, width), bf16),
            pltpu.VMEM((8, both, HEAD_DIM), bf16),
            pltpu.VMEM((8, rows, HEAD_DIM), bf16),
            pltpu.VMEM((WINDOW + 1, both, both), f32),
            pltpu.VMEM((WINDOW + 1, both, both), f32),
            pltpu.VMEM((both, 128), f32),
            pltpu.VMEM((both, both), f32),
            pltpu.VMEM((WINDOW + 1, 8, both), f32),
            pltpu.VMEM((WINDOW + 1, 2, 1, 128), f32),
            pltpu.VMEM((WINDOW + 1, 2, 1, 128), f32),
            pltpu.VMEM((WINDOW + 1, both, both), f32),
            pltpu.SemaphoreType.DMA((SEMS,)),
            pltpu.SemaphoreType.DMA((SEMS,)),
            pltpu.SemaphoreType.DMA((16,)),
        ],
        compiler_params=pltpu.CompilerParams(collective_id=0, has_side_effects=True),
    )(activations, conv_taps, gate_in.T, gate_out.T, queries, key_vectors, value_vectors, seg)


def solution(mesh):
    return jax.shard_map(
        per_device,
        mesh=mesh,
        in_specs=(
            P(("dp", "seq"), "heads"),
            P(None, "heads"),
            P("heads", "seq"),
            P(),
            P(("dp", "seq"), "heads"),
            P(("dp", "seq"), "heads"),
            P(("dp", "seq"), "heads"),
            P("dp"),
        ),
        out_specs=(P(("dp", "seq"), "heads"), P("heads", ("dp", "seq"))),
        check_vma=False,
    )
```

```python
import math

import jax
import jax.numpy as jnp
from jax import lax
from jax.experimental import pallas as pl
from jax.experimental.pallas import tpu as pltpu
from jax.sharding import PartitionSpec as P

MESH = pl.DeviceIdType.MESH
HEAD_DIM = 128
NEG = -1e30
LOG2E = math.log2(math.e)
SIDE = 4
CHIPS = SIDE * SIDE
WINDOW = 8
NT = (((1,), (1,)), ((), ()))

GATHER = 20
SEM_SWAP = 4 * GATHER
SEM_HALO = SEM_SWAP + 4
SEM_Z = SEM_HALO + 2
SEM_LOGIT = SEM_Z + 12
SEM_RET = SEM_LOGIT + 8
SEM_MASS = SEM_RET + 16
SEM_OUT = SEM_MASS + 18
SEMS = SEM_OUT + 8


def kernel(
    act_ref, taps_ref, wt_ref, gout_ref, q_ref, k_ref, v_ref, seg_ref,
    att_ref, mass_ref,
    rows_buf, mixed, wg, part, gsel, zrecv, lrecv, rown, rall, kvg, qbuf, obuf, orecv, sbuf, tbuf, tops, rel,
    colacc, colout, krecv, added, send_sem, recv_sem, local_sem,
):
    seq = lax.axis_index("seq")
    h = lax.axis_index("heads")
    c = lax.rem(seq, 2)
    ch = seq // 2
    x = ch // SIDE
    y = lax.rem(ch, SIDE)
    other = 1 - c
    shard_rows = act_ref.shape[0]
    half_q = q_ref.shape[1] // 2
    depth = act_ref.shape[1] // 2

    def at_chip(chip, core):
        return {"seq": lax.rem(chip, CHIPS) * 2 + core}

    def at_xy(xx, yy):
        return {"seq": (lax.rem(xx, SIDE) * SIDE + lax.rem(yy, SIDE)) * 2 + c}

    partner = {"seq": ch * 2 + other}

    barrier = pltpu.get_barrier_semaphore()

    def greet(i, carry):
        pl.semaphore_signal(
            barrier, inc=1, device_id={"seq": lax.rem(seq + i, 2 * CHIPS)}, device_id_type=MESH
        )
        return carry

    lax.fori_loop(1, 2 * CHIPS, greet, 0)
    for j in range(1, 4):
        for core in range(2):
            pl.semaphore_signal(
                barrier, inc=1, device_id={"seq": ch * 2 + core, "heads": lax.rem(h + j, 4)},
                device_id_type=MESH,
            )
    def columns(which, width):
        return pl.ds(pl.multiple_of(which * width, width), width)

    own_rows = pl.ds(pl.multiple_of(c * shard_rows, 128), shard_rows)
    own_rows_in = pl.ds(pl.multiple_of(c * shard_rows + 16, 16), shard_rows)

    def place(t, i):
        own = x if t == 0 else y
        return lax.rem(own + (0, 3, 1, 2)[i], SIDE)

    def wslot(t, d, i, ab=None):
        p = place(t, i)
        if ab is None:
            return wg.at[d, t, p]
        return wg.at[d, t, p, :, ab * depth : (ab + 1) * depth]

    def kvslot(t, d, i, ab=None):
        p = place(t, i)
        return kvg.at[t, d, p] if ab is None else kvg.at[t, d, p, ab]

    local = [
        pltpu.make_async_copy(act_ref, rows_buf.at[own_rows_in], local_sem.at[0]),
        pltpu.make_async_copy(wt_ref.at[0:16], wslot(0, 0, 0), local_sem.at[1]),
        pltpu.make_async_copy(wt_ref.at[16:32], wslot(1, 0, 0), local_sem.at[2]),
        pltpu.make_async_copy(k_ref.at[:, columns(c, 128)], kvg.at[0, 0, x, c], local_sem.at[3]),
        pltpu.make_async_copy(v_ref.at[:, columns(c, 128)], kvg.at[1, 0, y, c], local_sem.at[4]),
        pltpu.make_async_copy(q_ref.at[:, columns(c, half_q)], qbuf.at[own_rows], local_sem.at[5]),
    ]
    for copy in local:
        copy.start()

    rows = 2 * shard_rows
    pos = (ch * rows + lax.broadcasted_iota(jnp.int32, (rows, rows), 0)).astype(jnp.float32)
    first = jnp.zeros((rows, rows), jnp.float32)
    seg = seg_ref[...]
    for number in range(1, 4):
        count = jnp.sum((seg < number).astype(jnp.float32), axis=1, keepdims=True)
        count = jnp.sum(count, axis=0, keepdims=True)
        first = jnp.where(pos >= count, jnp.maximum(first, count), first)
    rel[...] = first - lax.broadcasted_iota(jnp.int32, (rows, rows), 1).astype(jnp.float32)
    colacc[...] = jnp.zeros_like(colacc)

    lane = lax.broadcasted_iota(jnp.int32, (1, 128), 1)
    kind, which, unit = lane // 64, lax.rem(lane // 16, SIDE), lax.rem(lane, 16)
    for d in range(SIDE):
        place_x = jnp.where(kind == 0, which, lax.rem(x + d, SIDE))
        place_y = jnp.where(kind == 0, lax.rem(y + d, SIDE), which)
        column = ((place_x * SIDE + place_y) * 2 + c) * 32 + kind * 16 + unit
        pick = lax.broadcasted_iota(jnp.int32, (gout_ref.shape[1], 128), 0) == column
        pick = jnp.where(pick, 1.0, 0.0).astype(jnp.bfloat16)
        chosen = jnp.dot(gout_ref[...], pick, preferred_element_type=jnp.float32)
        gsel[d] = chosen.astype(jnp.bfloat16)

    pl.semaphore_wait(barrier, 2 * CHIPS - 1 + 6)

    pending = []

    def send(src, dst, sem, device, rsem=None):
        copy = pltpu.make_async_remote_copy(
            src_ref=src, dst_ref=dst, send_sem=send_sem.at[sem],
            recv_sem=recv_sem.at[sem if rsem is None else rsem],
            device_id=device, device_id_type=MESH,
        )
        copy.start()
        pending.append(copy)

    def recv(slot, sem):
        pltpu.make_async_remote_copy(
            src_ref=slot, dst_ref=slot, send_sem=send_sem.at[sem], recv_sem=recv_sem.at[sem],
            device_id=partner, device_id_type=MESH,
        ).wait_recv()

    def axis_one(t, step):
        return at_xy(x + step, y) if t == 0 else at_xy(x, y + step)

    def axis_two(t, step):
        return at_xy(x, y + step) if t == 0 else at_xy(x + step, y)

    def second_sends(slot, base, t, i, src=None):
        source = slot(t, 0, i) if src is None else src
        sem = base + t * GATHER + 4 + 4 * i
        send(source, slot(t, 3, i), sem, axis_two(t, 1))
        send(source, slot(t, 1, i), sem + 1, axis_two(t, 3))

    def gather_start(slot, base, source):
        for t in range(2):
            sem = base + t * GATHER
            send(source(t), slot(t, 0, 0), sem, axis_one(t, 1))
            send(source(t), slot(t, 0, 0), sem + 1, axis_one(t, 3))
        for t in range(2):
            second_sends(slot, base, t, 0, source(t))

    def gather_first(slot, base, between=None):
        for t in range(2):
            sem = base + t * GATHER
            recv(slot(t, 0, 1), sem)
            send(slot(t, 0, 1, 0), slot(t, 0, 1, 0), sem + 2, axis_one(t, 1))
            recv(slot(t, 0, 2), sem + 1)
            send(slot(t, 0, 2, 1), slot(t, 0, 2, 1), sem + 3, axis_one(t, 3))
        for i in (1, 2):
            for t in range(2):
                second_sends(slot, base, t, i)
        if between is not None:
            between()
        for t in range(2):
            sem = base + t * GATHER
            recv(slot(t, 0, 3, 0), sem + 2)
            recv(slot(t, 0, 3, 1), sem + 3)
            second_sends(slot, base, t, 3)

    def gather_second(slot, base):
        for i in range(4):
            for t in range(2):
                sem = base + t * GATHER + 4 + 4 * i
                recv(slot(t, 3, i), sem)
                send(slot(t, 3, i, 0), slot(t, 2, i, 0), sem + 2, axis_two(t, 1))
                recv(slot(t, 1, i), sem + 1)
                send(slot(t, 1, i, 1), slot(t, 2, i, 1), sem + 3, axis_two(t, 3))

    def gather_last(slot, base):
        for i in range(4):
            for t in range(2):
                sem = base + t * GATHER + 4 + 4 * i
                recv(slot(t, 2, i, 0), sem + 2)
                recv(slot(t, 2, i, 1), sem + 3)

    W_BASE, KV_BASE = 0, 2 * GATHER
    @pl.when((c == 1) & (ch < CHIPS - 1))
    def _():
        for core in range(2):
            pltpu.make_async_remote_copy(
                src_ref=act_ref.at[shard_rows - 16 : shard_rows], dst_ref=rows_buf.at[0:16],
                send_sem=send_sem.at[SEM_HALO + core], recv_sem=recv_sem.at[SEM_HALO],
                device_id=at_chip(ch + 1, core), device_id_type=MESH,
            ).start()

    gather_start(wslot, W_BASE, lambda t: wt_ref.at[16 * t : 16 * t + 16])

    send(act_ref, rows_buf.at[own_rows_in], SEM_SWAP, partner)

    send(k_ref.at[:, columns(other, 128)], kvg.at[0, 0, x, c], SEM_SWAP + 2, partner)
    send(v_ref.at[:, columns(other, 128)], kvg.at[1, 0, y, c], SEM_SWAP + 3, partner)
    send(q_ref.at[:, columns(other, half_q)], qbuf.at[own_rows], SEM_SWAP + 1, partner)
    def convolve():
        @pl.when(ch > 0)
        def _():
            recv(rows_buf.at[0:16], SEM_HALO)

        recv(rows_buf.at[pl.ds(pl.multiple_of(other * shard_rows + 16, 16), shard_rows)], SEM_SWAP)
        for copy in local:
            copy.wait()

        @pl.when(ch == 0)
        def _():
            rows_buf[0:16, :] = jnp.zeros((16, rows_buf.shape[1]), jnp.bfloat16)

        width = 512
        tap_count = taps_ref.shape[0]

        def mix(step, carry):
            r0 = pl.multiple_of((step // 4) * 64, 64)
            cols = pl.ds(pl.multiple_of(lax.rem(step, 4) * width, width), width)
            block = rows_buf[pl.ds(r0, 80), cols].astype(jnp.float32)
            total = jnp.zeros((64, width), jnp.float32)
            for tap in range(tap_count):
                moved = block if tap == 0 else pltpu.roll(block, tap, axis=0)
                total = total + taps_ref[tap : tap + 1, cols].astype(jnp.float32) * moved[16:80]
            mixed[pl.ds(r0, 64), cols] = total.astype(jnp.bfloat16)
            return carry

        lax.fori_loop(0, (2 * shard_rows // 64) * (mixed.shape[1] // width), mix, 0)

    gather_first(wslot, W_BASE, convolve)

    def gate_group(d):
        total = lax.dot_general(
            mixed[...], wg[d].reshape(128, mixed.shape[1]), NT, preferred_element_type=jnp.float32
        )
        part[d] = total
        for j in range(1, 4):
            peer = lax.rem(h + j, 4)
            send(
                part.at[d, pl.ds(pl.multiple_of(peer * 64, 64), 64)], zrecv.at[d, j - 1],
                SEM_Z + 3 * d + j - 1, {"heads": peer},
            )

    gate_group(0)
    gather_second(wslot, W_BASE)

    recv(kvg.at[0, 0, x, other], SEM_SWAP + 2)
    recv(kvg.at[1, 0, y, other], SEM_SWAP + 3)
    gather_start(kvslot, KV_BASE, lambda t: kvslot(t, 0, 0))

    gate_group(3)
    gate_group(1)
    gather_last(wslot, W_BASE)
    gate_group(2)

    gather_first(kvslot, KV_BASE)

    logits = jnp.zeros((8, 64), jnp.float32)
    for d in (0, 3, 1, 2):
        for j in range(3):
            recv(zrecv.at[d, j], SEM_Z + 3 * d + j)
        pre = part[d, pl.ds(pl.multiple_of(h * 64, 64), 64), :]
        for j in range(3):
            pre = pre + zrecv[d, j]
        hidden = (pre / (1.0 + jnp.exp(-pre))).astype(jnp.bfloat16)
        logits = logits + lax.dot_general(gsel[d], hidden, NT, preferred_element_type=jnp.float32)
    mine = 2 * h + c
    lrecv[mine] = jnp.concatenate([logits, jnp.zeros((8, 64), jnp.float32)], 1)
    for j in range(4):
        for flip in range(2):
            if j or flip:
                peer, core = lax.rem(h + j, 4), lax.rem(c + flip, 2)
                send(
                    lrecv.at[mine], lrecv.at[mine], SEM_LOGIT + 2 * j + flip,
                    {"seq": ch * 2 + core, "heads": peer},
                )

    gather_second(kvslot, KV_BASE)

    for j in range(4):
        for flip in range(2):
            if j or flip:
                peer, core = lax.rem(h + 4 - j, 4), lax.rem(c + flip, 2)
                recv(lrecv.at[2 * peer + core], SEM_LOGIT + 2 * j + flip)
    lane = lax.broadcasted_iota(jnp.int32, (8, 128), 1)
    for block in range(2):
        low = lrecv[4 * block] + lrecv[4 * block + 1]
        high = pltpu.roll(lrecv[4 * block + 2] + lrecv[4 * block + 3], 64, axis=1)
        value = jnp.where(lane < 64, low, high)
        sig = jnp.minimum(value, 0.0) - jnp.log1p(jnp.exp(-jnp.abs(value)))
        rown[block] = sig.astype(jnp.bfloat16).astype(jnp.float32)
    for block in range(2):
        rall[ch, block : block + 1, :] = rown[block, pl.ds(mine, 1), :]
    for i in range(1, CHIPS):
        send(rall.at[ch], rall.at[ch], SEM_RET + i, at_chip(ch + i, c))

    gather_last(kvslot, KV_BASE)
    recv(qbuf.at[pl.ds(pl.multiple_of(other * shard_rows, 128), shard_rows)], SEM_SWAP + 1)

    for copy in pending:
        copy.wait_send()
    pending.clear()

    for i in range(1, CHIPS):
        recv(rall.at[lax.rem(ch + CHIPS - i, CHIPS)], SEM_RET + i)

    scale = LOG2E / math.sqrt(HEAD_DIM)
    blocks = range(WINDOW + 1)

    def chip_of(b):
        return lax.rem(ch + CHIPS - WINDOW + b, CHIPS)

    for b in blocks:
        bias = rall[chip_of(b)] * LOG2E
        start = ((ch - WINDOW + b) * rows).astype(jnp.float32)
        for half in range(2):
            lanes = slice(128 * half, 128 * half + 128)
            seen = rel[:, lanes] <= start
            if b == WINDOW:
                seen = seen & (
                    lax.broadcasted_iota(jnp.int32, (rows, 128), 1) + 128 * half
                    <= lax.broadcasted_iota(jnp.int32, (rows, 128), 0)
                )
            added[b, :, lanes] = jnp.where(seen, bias[half : half + 1], NEG)

    their_rows = pl.ds(pl.multiple_of(other * shard_rows, 128), shard_rows)

    def give(e):
        return pltpu.make_async_remote_copy(
            src_ref=obuf.at[e, their_rows], dst_ref=orecv.at[e],
            send_sem=send_sem.at[SEM_OUT + e], recv_sem=recv_sem.at[SEM_OUT + e],
            device_id=partner, device_id_type=MESH,
        )

    def key_block(kind, b):
        chip = chip_of(b)
        kx, ky = chip // SIDE, lax.rem(chip, SIDE)
        if kind == 0:
            block = kvg[0, lax.rem(ky + SIDE - y, SIDE), kx]
        else:
            block = kvg[1, lax.rem(kx + SIDE - x, SIDE), ky]
        return block.reshape(rows, HEAD_DIM)

    def query_of(e):
        return qbuf[:, pl.ds(pl.multiple_of(e * HEAD_DIM, HEAD_DIM), HEAD_DIM)]

    def score(query, slot, b, peak):
        scores = lax.dot_general(query, key_block(0, b), NT, preferred_element_type=jnp.float32)
        scores = scores * scale + added[b]
        slot[b] = scores
        return jnp.maximum(peak, jnp.maximum(scores[:, :128], scores[:, 128:]))

    def soften(slot, b, top, mass):
        piece = jnp.exp2(slot[b] - top)
        slot[b] = piece
        return mass + (piece[:, :128] + piece[:, 128:])

    def spread(slot, b, inverse, out):
        weights = slot[b] * inverse
        colacc[b] += jnp.sum(weights.reshape(rows // 8, 8, rows), axis=0)
        return out + jnp.dot(
            weights.astype(jnp.bfloat16), key_block(1, b), preferred_element_type=jnp.float32
        )

    low = jnp.full((rows, 128), NEG, jnp.float32)
    none = jnp.zeros((rows, 128), jnp.float32)

    def finish(e, slot, inverse):
        out = none
        for b in blocks:
            out = spread(slot, b, inverse, out)
        obuf[e] = out.astype(jnp.bfloat16)
        give(e).start()
        att_ref[:, columns(8 * c + e, HEAD_DIM)] = obuf[e, own_rows, :]

    def widest(peak):
        tops[...] = jnp.broadcast_to(jnp.max(peak, axis=1, keepdims=True), (rows, 128))

    peak = low
    query = query_of(0)
    for b in blocks:
        peak = score(query, sbuf, b, peak)
    widest(peak)
    head_count = half_q // HEAD_DIM

    def head_pair(pair, carry):
        for i, slot, following in ((0, sbuf, tbuf), (1, tbuf, sbuf)):
            e = 2 * pair + i
            top = tops[:, :1]
            query = query_of(jnp.minimum(e + 1, head_count - 1))
            peak, mass = low, none
            for b in blocks:
                peak = score(query, following, b, peak)
                mass = soften(slot, b, top, mass)
            finish(e, slot, 1.0 / jnp.sum(mass, axis=1, keepdims=True))
            widest(peak)
        return carry

    lax.fori_loop(0, head_count // 2, head_pair, 0)

    for b in blocks:
        total = jnp.sum(colacc[b], axis=0, keepdims=True)
        for half in range(2):
            colout[b, half] = total[:, 128 * half : 128 * half + 128]
    for b in range(WINDOW):
        for half in range(2):
            send(
                colout.at[b, half], krecv.at[b, c], SEM_MASS + 2 * b + half,
                at_chip(ch + CHIPS - WINDOW + b, half), SEM_MASS + 2 * b + c,
            )
    send(
        colout.at[WINDOW, other], krecv.at[WINDOW, c], SEM_MASS + 2 * WINDOW + other, partner,
        SEM_MASS + 2 * WINDOW + c,
    )
    krecv[WINDOW, c] = colout[WINDOW, c]
    for e in range(half_q // HEAD_DIM):
        give(e).wait()
        att_ref[:, columns(8 * other + e, HEAD_DIM)] = orecv[e]

    for b in range(WINDOW):
        for core in range(2):
            recv(krecv.at[b, core], SEM_MASS + 2 * b + core)
    recv(krecv.at[WINDOW, other], SEM_MASS + 2 * WINDOW + other)
    for core in range(2):
        total = krecv[0, core]
        for b in range(1, WINDOW + 1):
            total = total + krecv[b, core]
        mass_ref[core : core + 1, :] = (total / 8.0).astype(jnp.bfloat16)

    for copy in pending:
        copy.wait_send()

    @pl.when((c == 1) & (ch < CHIPS - 1))
    def _():
        for core in range(2):
            pltpu.make_async_remote_copy(
                src_ref=act_ref.at[shard_rows - 16 : shard_rows], dst_ref=rows_buf.at[0:16],
                send_sem=send_sem.at[SEM_HALO + core], recv_sem=recv_sem.at[SEM_HALO],
                device_id=at_chip(ch + 1, core), device_id_type=MESH,
            ).wait_send()


def per_device(
    activations, conv_taps, gate_in, gate_out, queries, key_vectors, value_vectors, segment_ids
):
    rows, features = activations.shape
    seg = segment_ids.reshape(-1, 128)
    width = queries.shape[1] // 2
    vmem = pl.BlockSpec(memory_space=pltpu.VMEM)
    anywhere = pl.BlockSpec(memory_space=pl.ANY)
    both = 2 * rows
    bf16, f32 = jnp.bfloat16, jnp.float32
    return pl.pallas_call(
        kernel,
        name="retention_step",
        out_shape=(
            pltpu.VMEM((rows, 2 * width), bf16),
            pltpu.VMEM((2, rows), bf16),
        ),
        in_specs=[anywhere, vmem, anywhere, vmem, anywhere, anywhere, anywhere, vmem],
        out_specs=(vmem, vmem),
        scratch_shapes=[
            pltpu.VMEM((both + 16, features), bf16),
            pltpu.VMEM((both, features), bf16),
            pltpu.VMEM((SIDE, 2, SIDE, 16, features), bf16),
            pltpu.VMEM((SIDE, both, 128), f32),
            pltpu.VMEM((SIDE, 8, 128), bf16),
            pltpu.VMEM((SIDE, 3, 64, 128), f32),
            pltpu.VMEM((8, 8, 128), f32),
            pltpu.VMEM((2, 8, 128), f32),
            pltpu.VMEM((CHIPS, 2, 128), f32),
            pltpu.VMEM((2, SIDE, SIDE, 2, rows, HEAD_DIM), bf16),
            pltpu.VMEM((both, width), bf16),
            pltpu.VMEM((8, both, HEAD_DIM), bf16),
            pltpu.VMEM((8, rows, HEAD_DIM), bf16),
            pltpu.VMEM((WINDOW + 1, both, both), f32),
            pltpu.VMEM((WINDOW + 1, both, both), f32),
            pltpu.VMEM((both, 128), f32),
            pltpu.VMEM((both, both), f32),
            pltpu.VMEM((WINDOW + 1, 8, both), f32),
            pltpu.VMEM((WINDOW + 1, 2, 1, 128), f32),
            pltpu.VMEM((WINDOW + 1, 2, 1, 128), f32),
            pltpu.VMEM((WINDOW + 1, both, both), f32),
            pltpu.SemaphoreType.DMA((SEMS,)),
            pltpu.SemaphoreType.DMA((SEMS,)),
            pltpu.SemaphoreType.DMA((6,)),
        ],
        compiler_params=pltpu.CompilerParams(collective_id=0, has_side_effects=True),
    )(activations, conv_taps, gate_in.T, gate_out.T, queries, key_vectors, value_vectors, seg)


def solution(mesh):
    return jax.shard_map(
        per_device,
        mesh=mesh,
        in_specs=(
            P(("dp", "seq"), "heads"),
            P(None, "heads"),
            P("heads", "seq"),
            P(),
            P(("dp", "seq"), "heads"),
            P(("dp", "seq"), "heads"),
            P(("dp", "seq"), "heads"),
            P("dp"),
        ),
        out_specs=(P(("dp", "seq"), "heads"), P("heads", ("dp", "seq"))),
        check_vma=False,
    )
```

```python
import math

import jax
import jax.numpy as jnp
from jax import lax
from jax.experimental import pallas as pl
from jax.experimental.pallas import tpu as pltpu
from jax.sharding import PartitionSpec as P

MESH = pl.DeviceIdType.MESH
HEAD_DIM = 128
NEG = -1e30
LOG2E = math.log2(math.e)
SIDE = 4
CHIPS = SIDE * SIDE
WINDOW = 8
NT = (((1,), (1,)), ((), ()))

GATHER = 20
SEM_SWAP = 4 * GATHER
SEM_HALO = SEM_SWAP + 4
SEM_Z = SEM_HALO + 2
SEM_LOGIT = SEM_Z + 12
SEM_RET = SEM_LOGIT + 8
SEM_MASS = SEM_RET + 16
SEM_OUT = SEM_MASS + 18
SEMS = SEM_OUT + 8


def kernel(
    act_ref, taps_ref, wt_ref, gout_ref, q_ref, k_ref, v_ref, seg_ref,
    att_ref, mass_ref,
    rows_buf, mixed, wg, part, gsel, zrecv, lrecv, rown, rall, kvg, qbuf, obuf, orecv, sbuf, tbuf, tops, rel,
    colacc, colout, krecv, added, send_sem, recv_sem, local_sem,
):
    seq = lax.axis_index("seq")
    h = lax.axis_index("heads")
    c = lax.rem(seq, 2)
    ch = seq // 2
    x = ch // SIDE
    y = lax.rem(ch, SIDE)
    other = 1 - c
    shard_rows = act_ref.shape[0]
    half_q = q_ref.shape[1] // 2
    depth = act_ref.shape[1] // 2

    def at_chip(chip, core):
        return {"seq": lax.rem(chip, CHIPS) * 2 + core}

    def at_xy(xx, yy):
        return {"seq": (lax.rem(xx, SIDE) * SIDE + lax.rem(yy, SIDE)) * 2 + c}

    partner = {"seq": ch * 2 + other}

    barrier = pltpu.get_barrier_semaphore()

    def greet(i, carry):
        pl.semaphore_signal(
            barrier, inc=1, device_id={"seq": lax.rem(seq + i, 2 * CHIPS)}, device_id_type=MESH
        )
        return carry

    lax.fori_loop(1, 2 * CHIPS, greet, 0)
    for j in range(1, 4):
        for core in range(2):
            pl.semaphore_signal(
                barrier, inc=1, device_id={"seq": ch * 2 + core, "heads": lax.rem(h + j, 4)},
                device_id_type=MESH,
            )
    def columns(which, width):
        return pl.ds(pl.multiple_of(which * width, width), width)

    own_rows = pl.ds(pl.multiple_of(c * shard_rows, 128), shard_rows)
    own_rows_in = pl.ds(pl.multiple_of(c * shard_rows + 16, 16), shard_rows)

    def place(t, i):
        own = x if t == 0 else y
        return lax.rem(own + (0, 3, 1, 2)[i], SIDE)

    def wslot(t, d, i, ab=None):
        p = place(t, i)
        if ab is None:
            return wg.at[d, t, p]
        return wg.at[d, t, p, :, ab * depth : (ab + 1) * depth]

    def kvslot(t, d, i, ab=None):
        p = place(t, i)
        return kvg.at[t, d, p] if ab is None else kvg.at[t, d, p, ab]

    local = [
        pltpu.make_async_copy(act_ref, rows_buf.at[own_rows_in], local_sem.at[0]),
        pltpu.make_async_copy(wt_ref.at[0:16], wslot(0, 0, 0), local_sem.at[1]),
        pltpu.make_async_copy(wt_ref.at[16:32], wslot(1, 0, 0), local_sem.at[2]),
        pltpu.make_async_copy(k_ref.at[:, columns(c, 128)], kvg.at[0, 0, x, c], local_sem.at[3]),
        pltpu.make_async_copy(v_ref.at[:, columns(c, 128)], kvg.at[1, 0, y, c], local_sem.at[4]),
        pltpu.make_async_copy(q_ref.at[:, columns(c, half_q)], qbuf.at[own_rows], local_sem.at[5]),
    ]
    for copy in local:
        copy.start()

    rows = 2 * shard_rows
    pos = (ch * rows + lax.broadcasted_iota(jnp.int32, (rows, rows), 0)).astype(jnp.float32)
    first = jnp.zeros((rows, rows), jnp.float32)
    seg = seg_ref[...]
    for number in range(1, 4):
        count = jnp.sum((seg < number).astype(jnp.float32), axis=1, keepdims=True)
        count = jnp.sum(count, axis=0, keepdims=True)
        first = jnp.where(pos >= count, jnp.maximum(first, count), first)
    rel[...] = first - lax.broadcasted_iota(jnp.int32, (rows, rows), 1).astype(jnp.float32)
    colacc[...] = jnp.zeros_like(colacc)

    lane = lax.broadcasted_iota(jnp.int32, (1, 128), 1)
    kind, which, unit = lane // 64, lax.rem(lane // 16, SIDE), lax.rem(lane, 16)
    for d in range(SIDE):
        place_x = jnp.where(kind == 0, which, lax.rem(x + d, SIDE))
        place_y = jnp.where(kind == 0, lax.rem(y + d, SIDE), which)
        column = ((place_x * SIDE + place_y) * 2 + c) * 32 + kind * 16 + unit
        pick = lax.broadcasted_iota(jnp.int32, (gout_ref.shape[1], 128), 0) == column
        pick = jnp.where(pick, 1.0, 0.0).astype(jnp.bfloat16)
        chosen = jnp.dot(gout_ref[...], pick, preferred_element_type=jnp.float32)
        gsel[d] = chosen.astype(jnp.bfloat16)

    pl.semaphore_wait(barrier, 2 * CHIPS - 1 + 6)

    pending = []

    def send(src, dst, sem, device, rsem=None):
        copy = pltpu.make_async_remote_copy(
            src_ref=src, dst_ref=dst, send_sem=send_sem.at[sem],
            recv_sem=recv_sem.at[sem if rsem is None else rsem],
            device_id=device, device_id_type=MESH,
        )
        copy.start()
        pending.append(copy)

    def recv(slot, sem):
        pltpu.make_async_remote_copy(
            src_ref=slot, dst_ref=slot, send_sem=send_sem.at[sem], recv_sem=recv_sem.at[sem],
            device_id=partner, device_id_type=MESH,
        ).wait_recv()

    def axis_one(t, step):
        return at_xy(x + step, y) if t == 0 else at_xy(x, y + step)

    def axis_two(t, step):
        return at_xy(x, y + step) if t == 0 else at_xy(x + step, y)

    def unseen(base, t, i):
        return base == 2 * GATHER and t == 0 and i == 2

    def left_part(base, t):
        return 1 if base == 2 * GATHER and t == 1 else None

    def second_sends(slot, base, t, i, src=None):
        if unseen(base, t, i):
            return
        source = slot(t, 0, i) if src is None else src
        sem = base + t * GATHER + 4 + 4 * i
        send(source, slot(t, 3, i), sem, axis_two(t, 1))
        part_left = left_part(base, t)
        if part_left is not None:
            source = slot(t, 0, i, part_left)
        send(source, slot(t, 1, i, part_left), sem + 1, axis_two(t, 3))

    def gather_start(slot, base, source):
        for t in range(2):
            sem = base + t * GATHER
            send(source(t), slot(t, 0, 0), sem, axis_one(t, 1))
            send(source(t), slot(t, 0, 0), sem + 1, axis_one(t, 3))
        for t in range(2):
            second_sends(slot, base, t, 0, source(t))

    def gather_first(slot, base, between=None):
        for t in range(2):
            sem = base + t * GATHER
            recv(slot(t, 0, 1), sem)
            send(slot(t, 0, 1, 0), slot(t, 0, 1, 0), sem + 2, axis_one(t, 1))
            recv(slot(t, 0, 2), sem + 1)
            send(slot(t, 0, 2, 1), slot(t, 0, 2, 1), sem + 3, axis_one(t, 3))
        for i in (1, 2):
            for t in range(2):
                second_sends(slot, base, t, i)
        if between is not None:
            between()
        for t in range(2):
            sem = base + t * GATHER
            recv(slot(t, 0, 3, 0), sem + 2)
            recv(slot(t, 0, 3, 1), sem + 3)
            second_sends(slot, base, t, 3)

    def gather_second(slot, base):
        for i in range(4):
            for t in range(2):
                if unseen(base, t, i):
                    continue
                sem = base + t * GATHER + 4 + 4 * i
                recv(slot(t, 3, i), sem)
                send(slot(t, 3, i, 0), slot(t, 2, i, 0), sem + 2, axis_two(t, 1))
                recv(slot(t, 1, i, left_part(base, t)), sem + 1)
                send(slot(t, 1, i, 1), slot(t, 2, i, 1), sem + 3, axis_two(t, 3))

    def gather_last(slot, base):
        for i in range(4):
            for t in range(2):
                if unseen(base, t, i):
                    continue
                sem = base + t * GATHER + 4 + 4 * i
                recv(slot(t, 2, i, 0), sem + 2)
                recv(slot(t, 2, i, 1), sem + 3)

    W_BASE, KV_BASE = 0, 2 * GATHER
    @pl.when((c == 1) & (ch < CHIPS - 1))
    def _():
        for core in range(2):
            pltpu.make_async_remote_copy(
                src_ref=act_ref.at[shard_rows - 16 : shard_rows], dst_ref=rows_buf.at[0:16],
                send_sem=send_sem.at[SEM_HALO + core], recv_sem=recv_sem.at[SEM_HALO],
                device_id=at_chip(ch + 1, core), device_id_type=MESH,
            ).start()

    gather_start(wslot, W_BASE, lambda t: wt_ref.at[16 * t : 16 * t + 16])

    send(act_ref, rows_buf.at[own_rows_in], SEM_SWAP, partner)

    send(k_ref.at[:, columns(other, 128)], kvg.at[0, 0, x, c], SEM_SWAP + 2, partner)
    send(v_ref.at[:, columns(other, 128)], kvg.at[1, 0, y, c], SEM_SWAP + 3, partner)
    send(q_ref.at[:, columns(other, half_q)], qbuf.at[own_rows], SEM_SWAP + 1, partner)
    def convolve():
        @pl.when(ch > 0)
        def _():
            recv(rows_buf.at[0:16], SEM_HALO)

        recv(rows_buf.at[pl.ds(pl.multiple_of(other * shard_rows + 16, 16), shard_rows)], SEM_SWAP)
        for copy in local:
            copy.wait()

        @pl.when(ch == 0)
        def _():
            rows_buf[0:16, :] = jnp.zeros((16, rows_buf.shape[1]), jnp.bfloat16)

        width = 512
        tap_count = taps_ref.shape[0]

        def mix(step, carry):
            r0 = pl.multiple_of((step // 4) * 64, 64)
            cols = pl.ds(pl.multiple_of(lax.rem(step, 4) * width, width), width)
            block = rows_buf[pl.ds(r0, 80), cols].astype(jnp.float32)
            total = jnp.zeros((64, width), jnp.float32)
            for tap in range(tap_count):
                moved = block if tap == 0 else pltpu.roll(block, tap, axis=0)
                total = total + taps_ref[tap : tap + 1, cols].astype(jnp.float32) * moved[16:80]
            mixed[pl.ds(r0, 64), cols] = total.astype(jnp.bfloat16)
            return carry

        lax.fori_loop(0, (2 * shard_rows // 64) * (mixed.shape[1] // width), mix, 0)

    gather_first(wslot, W_BASE, convolve)

    def gate_group(d):
        total = lax.dot_general(
            mixed[...], wg[d].reshape(128, mixed.shape[1]), NT, preferred_element_type=jnp.float32
        )
        part[d] = total
        for j in range(1, 4):
            peer = lax.rem(h + j, 4)
            send(
                part.at[d, pl.ds(pl.multiple_of(peer * 64, 64), 64)], zrecv.at[d, j - 1],
                SEM_Z + 3 * d + j - 1, {"heads": peer},
            )

    gate_group(0)
    gather_second(wslot, W_BASE)

    recv(kvg.at[0, 0, x, other], SEM_SWAP + 2)
    recv(kvg.at[1, 0, y, other], SEM_SWAP + 3)
    gather_start(kvslot, KV_BASE, lambda t: kvslot(t, 0, 0))

    gate_group(3)
    gate_group(1)
    gather_last(wslot, W_BASE)
    gate_group(2)

    gather_first(kvslot, KV_BASE)

    logits = jnp.zeros((8, 64), jnp.float32)
    for d in (0, 3, 1, 2):
        for j in range(3):
            recv(zrecv.at[d, j], SEM_Z + 3 * d + j)
        pre = part[d, pl.ds(pl.multiple_of(h * 64, 64), 64), :]
        for j in range(3):
            pre = pre + zrecv[d, j]
        hidden = (pre / (1.0 + jnp.exp(-pre))).astype(jnp.bfloat16)
        logits = logits + lax.dot_general(gsel[d], hidden, NT, preferred_element_type=jnp.float32)
    mine = 2 * h + c
    lrecv[mine] = jnp.concatenate([logits, jnp.zeros((8, 64), jnp.float32)], 1)
    for j in range(4):
        for flip in range(2):
            if j or flip:
                peer, core = lax.rem(h + j, 4), lax.rem(c + flip, 2)
                send(
                    lrecv.at[mine], lrecv.at[mine], SEM_LOGIT + 2 * j + flip,
                    {"seq": ch * 2 + core, "heads": peer},
                )

    gather_second(kvslot, KV_BASE)

    for j in range(4):
        for flip in range(2):
            if j or flip:
                peer, core = lax.rem(h + 4 - j, 4), lax.rem(c + flip, 2)
                recv(lrecv.at[2 * peer + core], SEM_LOGIT + 2 * j + flip)
    lane = lax.broadcasted_iota(jnp.int32, (8, 128), 1)
    for block in range(2):
        low = lrecv[4 * block] + lrecv[4 * block + 1]
        high = pltpu.roll(lrecv[4 * block + 2] + lrecv[4 * block + 3], 64, axis=1)
        value = jnp.where(lane < 64, low, high)
        sig = jnp.minimum(value, 0.0) - jnp.log1p(jnp.exp(-jnp.abs(value)))
        rown[block] = sig.astype(jnp.bfloat16).astype(jnp.float32)
    for block in range(2):
        rall[ch, block : block + 1, :] = rown[block, pl.ds(mine, 1), :]
    for i in range(1, CHIPS):
        send(rall.at[ch], rall.at[ch], SEM_RET + i, at_chip(ch + i, c))

    gather_last(kvslot, KV_BASE)
    recv(qbuf.at[pl.ds(pl.multiple_of(other * shard_rows, 128), shard_rows)], SEM_SWAP + 1)

    for copy in pending:
        copy.wait_send()
    pending.clear()

    for i in range(1, CHIPS):
        recv(rall.at[lax.rem(ch + CHIPS - i, CHIPS)], SEM_RET + i)

    scale = LOG2E / math.sqrt(HEAD_DIM)
    blocks = range(WINDOW + 1)

    def chip_of(b):
        return lax.rem(ch + CHIPS - WINDOW + b, CHIPS)

    for b in blocks:
        bias = rall[chip_of(b)] * LOG2E
        start = ((ch - WINDOW + b) * rows).astype(jnp.float32)
        for half in range(2):
            lanes = slice(128 * half, 128 * half + 128)
            seen = rel[:, lanes] <= start
            if b == WINDOW:
                seen = seen & (
                    lax.broadcasted_iota(jnp.int32, (rows, 128), 1) + 128 * half
                    <= lax.broadcasted_iota(jnp.int32, (rows, 128), 0)
                )
            added[b, :, lanes] = jnp.where(seen, bias[half : half + 1], NEG)

    their_rows = pl.ds(pl.multiple_of(other * shard_rows, 128), shard_rows)

    def give(e):
        return pltpu.make_async_remote_copy(
            src_ref=obuf.at[e, their_rows], dst_ref=orecv.at[e],
            send_sem=send_sem.at[SEM_OUT + e], recv_sem=recv_sem.at[SEM_OUT + e],
            device_id=partner, device_id_type=MESH,
        )

    def key_block(kind, b):
        chip = chip_of(b)
        kx, ky = chip // SIDE, lax.rem(chip, SIDE)
        if kind == 0:
            block = kvg[0, lax.rem(ky + SIDE - y, SIDE), kx]
        else:
            block = kvg[1, lax.rem(kx + SIDE - x, SIDE), ky]
        return block.reshape(rows, HEAD_DIM)

    def query_of(e):
        return qbuf[:, pl.ds(pl.multiple_of(e * HEAD_DIM, HEAD_DIM), HEAD_DIM)]

    def score(query, slot, b, peak):
        scores = lax.dot_general(query, key_block(0, b), NT, preferred_element_type=jnp.float32)
        scores = scores * scale + added[b]
        slot[b] = scores
        return jnp.maximum(peak, jnp.maximum(scores[:, :128], scores[:, 128:]))

    def soften(slot, b, top, mass):
        piece = jnp.exp2(slot[b] - top)
        slot[b] = piece
        return mass + (piece[:, :128] + piece[:, 128:])

    def spread(slot, b, inverse, out):
        weights = slot[b] * inverse
        colacc[b] += jnp.sum(weights.reshape(rows // 8, 8, rows), axis=0)
        return out + jnp.dot(
            weights.astype(jnp.bfloat16), key_block(1, b), preferred_element_type=jnp.float32
        )

    low = jnp.full((rows, 128), NEG, jnp.float32)
    none = jnp.zeros((rows, 128), jnp.float32)

    def finish(e, slot, inverse):
        out = none
        for b in blocks:
            out = spread(slot, b, inverse, out)
        obuf[e] = out.astype(jnp.bfloat16)
        give(e).start()
        att_ref[:, columns(8 * c + e, HEAD_DIM)] = obuf[e, own_rows, :]

    def widest(peak):
        tops[...] = jnp.broadcast_to(jnp.max(peak, axis=1, keepdims=True), (rows, 128))

    peak = low
    query = query_of(0)
    for b in blocks:
        peak = score(query, sbuf, b, peak)
    widest(peak)
    head_count = half_q // HEAD_DIM

    def head_pair(pair, carry):
        for i, slot, following in ((0, sbuf, tbuf), (1, tbuf, sbuf)):
            e = 2 * pair + i
            top = tops[:, :1]
            query = query_of(jnp.minimum(e + 1, head_count - 1))
            peak, mass = low, none
            for b in blocks:
                peak = score(query, following, b, peak)
                mass = soften(slot, b, top, mass)
            finish(e, slot, 1.0 / jnp.sum(mass, axis=1, keepdims=True))
            widest(peak)
        return carry

    lax.fori_loop(0, head_count // 2, head_pair, 0)

    for b in blocks:
        total = jnp.sum(colacc[b], axis=0, keepdims=True)
        for half in range(2):
            colout[b, half] = total[:, 128 * half : 128 * half + 128]
    for b in range(WINDOW):
        for half in range(2):
            send(
                colout.at[b, half], krecv.at[b, c], SEM_MASS + 2 * b + half,
                at_chip(ch + CHIPS - WINDOW + b, half), SEM_MASS + 2 * b + c,
            )
    send(
        colout.at[WINDOW, other], krecv.at[WINDOW, c], SEM_MASS + 2 * WINDOW + other, partner,
        SEM_MASS + 2 * WINDOW + c,
    )
    krecv[WINDOW, c] = colout[WINDOW, c]
    for e in range(half_q // HEAD_DIM):
        give(e).wait()
        att_ref[:, columns(8 * other + e, HEAD_DIM)] = orecv[e]

    for b in range(WINDOW):
        for core in range(2):
            recv(krecv.at[b, core], SEM_MASS + 2 * b + core)
    recv(krecv.at[WINDOW, other], SEM_MASS + 2 * WINDOW + other)
    for core in range(2):
        total = krecv[0, core]
        for b in range(1, WINDOW + 1):
            total = total + krecv[b, core]
        mass_ref[core : core + 1, :] = (total / 8.0).astype(jnp.bfloat16)

    for copy in pending:
        copy.wait_send()

    @pl.when((c == 1) & (ch < CHIPS - 1))
    def _():
        for core in range(2):
            pltpu.make_async_remote_copy(
                src_ref=act_ref.at[shard_rows - 16 : shard_rows], dst_ref=rows_buf.at[0:16],
                send_sem=send_sem.at[SEM_HALO + core], recv_sem=recv_sem.at[SEM_HALO],
                device_id=at_chip(ch + 1, core), device_id_type=MESH,
            ).wait_send()


def per_device(
    activations, conv_taps, gate_in, gate_out, queries, key_vectors, value_vectors, segment_ids
):
    rows, features = activations.shape
    seg = segment_ids.reshape(-1, 128)
    width = queries.shape[1] // 2
    vmem = pl.BlockSpec(memory_space=pltpu.VMEM)
    anywhere = pl.BlockSpec(memory_space=pl.ANY)
    both = 2 * rows
    bf16, f32 = jnp.bfloat16, jnp.float32
    return pl.pallas_call(
        kernel,
        name="retention_step",
        out_shape=(
            pltpu.VMEM((rows, 2 * width), bf16),
            pltpu.VMEM((2, rows), bf16),
        ),
        in_specs=[anywhere, vmem, anywhere, vmem, anywhere, anywhere, anywhere, vmem],
        out_specs=(vmem, vmem),
        scratch_shapes=[
            pltpu.VMEM((both + 16, features), bf16),
            pltpu.VMEM((both, features), bf16),
            pltpu.VMEM((SIDE, 2, SIDE, 16, features), bf16),
            pltpu.VMEM((SIDE, both, 128), f32),
            pltpu.VMEM((SIDE, 8, 128), bf16),
            pltpu.VMEM((SIDE, 3, 64, 128), f32),
            pltpu.VMEM((8, 8, 128), f32),
            pltpu.VMEM((2, 8, 128), f32),
            pltpu.VMEM((CHIPS, 2, 128), f32),
            pltpu.VMEM((2, SIDE, SIDE, 2, rows, HEAD_DIM), bf16),
            pltpu.VMEM((both, width), bf16),
            pltpu.VMEM((8, both, HEAD_DIM), bf16),
            pltpu.VMEM((8, rows, HEAD_DIM), bf16),
            pltpu.VMEM((WINDOW + 1, both, both), f32),
            pltpu.VMEM((WINDOW + 1, both, both), f32),
            pltpu.VMEM((both, 128), f32),
            pltpu.VMEM((both, both), f32),
            pltpu.VMEM((WINDOW + 1, 8, both), f32),
            pltpu.VMEM((WINDOW + 1, 2, 1, 128), f32),
            pltpu.VMEM((WINDOW + 1, 2, 1, 128), f32),
            pltpu.VMEM((WINDOW + 1, both, both), f32),
            pltpu.SemaphoreType.DMA((SEMS,)),
            pltpu.SemaphoreType.DMA((SEMS,)),
            pltpu.SemaphoreType.DMA((6,)),
        ],
        compiler_params=pltpu.CompilerParams(collective_id=0, has_side_effects=True),
    )(activations, conv_taps, gate_in.T, gate_out.T, queries, key_vectors, value_vectors, seg)


def solution(mesh):
    return jax.shard_map(
        per_device,
        mesh=mesh,
        in_specs=(
            P(("dp", "seq"), "heads"),
            P(None, "heads"),
            P("heads", "seq"),
            P(),
            P(("dp", "seq"), "heads"),
            P(("dp", "seq"), "heads"),
            P(("dp", "seq"), "heads"),
            P("dp"),
        ),
        out_specs=(P(("dp", "seq"), "heads"), P("heads", ("dp", "seq"))),
        check_vma=False,
    )
```
